32 devices in a mesh: rep: 4 (over x, core), fsdp: 8 (over z, y).
Axes of the slice: x: 2, y: 2, z: 4, core: 2. Of those that a mesh axis runs over, the one named last changes fastest.
Arguments:
- tokens: bfloat16 [4, 1024, 2048], P('rep', 'fsdp'), may hold values from -6 to 6
- w_up: bfloat16 [4, 2048, 8192], P('rep', 'fsdp'), may hold values from -0.125 to 0.125
- d_out: bfloat16 [4, 1024, 8192], P('rep', 'fsdp'), may hold values from -1 to 1
- round_k: int32 [8], P('fsdp'), may hold values from 0 to 1
Outputs:
- block_out: bfloat16 [4, 1024, 8192], P('rep', 'fsdp')
- grad_up: float32 [4, 2048, 8192], P('rep', 'fsdp')
The draws below stay inside these ranges and needn't reach their ends.
All inputs are finite; a program needn't handle non-finite values.
Results may differ from the reference program's by a relative error of at most 0.01.
Values may be sent and summed in bfloat16 or wider, within the bound.
No kernel may reach another device: no remote copies, remote signals or barrier semaphores. Data moves between devices by JAX's collectives and lax.ppermute only.
A program may use at most 192 MiB of HBM per device.

```python
import jax
import jax.numpy as jnp
from jax import lax

D = 2048
FF = 8192
TOK_DEV = 128
LOG_REP = 2
REPS = 4
SHARDS = 8
TOKENS = 1024
N_FSDP = 8


def set_ends(result, own_key, low, top_value):
    spot = [jax.random.randint(jax.random.fold_in(own_key, axis), (), 0, length) for axis, length in enumerate(result.shape)]
    longest = result.shape.index(max(result.shape))
    beside = spot[:longest] + [(spot[longest] + 1) % result.shape[longest]] + spot[longest + 1:]
    return result.at[tuple(spot)].set(low).at[tuple(beside)].set(top_value)


def steps_of(key, extent, shards, low, high):
    level, own = 1.0, jax.random.fold_in(key, 6)
    for axis_at, parts in shards:
        heights = jnp.exp(jax.random.uniform(jax.random.fold_in(own, axis_at), (parts,), jnp.float32, low / len(shards), high / len(shards)))
        level = level * jnp.repeat(heights, extent[axis_at] // parts).reshape([-1 if axis == axis_at else 1 for axis in range(len(extent))])
    return level


def noise(own_key, dims, scale, bound, pieces=(), held_as=jnp.bfloat16):
    values = jax.random.normal(own_key, dims, jnp.float32) * scale
    if len(pieces) > 0:
        values = steps_of(own_key, dims, pieces, -0.22, 0.18) * values
    return jnp.clip(values, min=-bound, max=bound).astype(held_as)


def setup_inputs(seed: int = 0) -> dict:
    key_of = jax.random.split(jax.random.key(seed), 5)
    tokens = noise(key_of[0], (REPS, TOKENS, D), 1.0, 6.0, ((0, 4), (1, 8)))
    w_up = noise(key_of[1], (REPS, D, FF), D ** -0.5, 0.125, ((0, 4), (1, 8)))
    d_out = noise(key_of[2], (REPS, TOKENS, FF), (2 * TOKENS ** -0.5), 1.0, ((0, 4), (1, 8)))
    round_k = set_ends(jax.random.randint(key_of[3], (SHARDS,), 0, LOG_REP), jax.random.fold_in(key_of[3], 1), 0, LOG_REP - 1).astype(jnp.int32)
    return {"tokens": tokens, "w_up": w_up, "d_out": d_out, "round_k": round_k}


def gelu_parts(pre):
    inner = 0.7978845608 * (pre + 0.044715 * pre * pre * pre)
    tanh_val = jnp.tanh(inner)
    act = 0.5 * pre * (1.0 + tanh_val)
    slope = 0.5 * (1.0 + tanh_val) + 0.5 * pre * (1.0 - tanh_val * tanh_val) * 0.7978845608 * (1.0 + 3.0 * 0.044715 * pre * pre)
    return act, slope


def block_sum(left, right):
    left_blocks = left.reshape(N_FSDP, TOK_DEV, left.shape[1])
    right_blocks = right.reshape(N_FSDP, TOK_DEV, right.shape[1])

    def step(total, pair):
        term = lax.dot_general(pair[0], pair[1], (((0,), (0,)), ((), ())), preferred_element_type=jnp.float32)
        term = lax.optimization_barrier(term.astype(jnp.bfloat16))
        return total + term.astype(jnp.float32), None

    init = jnp.zeros((left.shape[1], right.shape[1]), jnp.float32)
    total, _ = lax.scan(step, init, (left_blocks, right_blocks))
    return total


def averaged(weights, rank, shifts):
    blocks = weights.reshape(REPS, SHARDS, weights.shape[1] // SHARDS, weights.shape[2])
    other = blocks[rank]
    for bit in range(LOG_REP):
        chosen = (shifts == bit)[:, None, None]
        other = jnp.where(chosen, blocks[rank ^ (1 << bit)], other)
    mean = (blocks[rank].astype(jnp.float32) + other.astype(jnp.float32)) * 0.5
    return mean.astype(jnp.bfloat16).reshape(weights.shape[1], weights.shape[2])


def reference(tokens, w_up, d_out, round_k):
    shifts = round_k.astype(jnp.int32)
    outs_list, up_list = [], []
    for rank in range(REPS):
        avg_up = averaged(w_up, rank, shifts)
        inputs = tokens[rank]
        pre = jnp.dot(inputs, avg_up, preferred_element_type=jnp.float32)
        act, slope = gelu_parts(pre)
        outs_list.append(act.astype(jnp.bfloat16))
        d_pre = (d_out[rank].astype(jnp.float32) * slope).astype(jnp.bfloat16)
        up_list.append(block_sum(inputs, d_pre))
    return jnp.stack(outs_list), jnp.stack(up_list)
```

```python
import jax
import jax.numpy as jnp
from jax import lax
from jax.sharding import Mesh, PartitionSpec as P


BF16, F32 = jnp.bfloat16, jnp.float32
CHUNKS = 4


def gelu_parts(pre):
    inner = 0.7978845608 * (pre + 0.044715 * pre * pre * pre)
    tanh_val = jnp.tanh(inner)
    act = 0.5 * pre * (1.0 + tanh_val)
    slope = 0.5 * (1.0 + tanh_val) + 0.5 * pre * (1.0 - tanh_val * tanh_val) * 0.7978845608 * (
        1.0 + 3.0 * 0.044715 * pre * pre
    )
    return (act, slope)


def dot(a, b):
    return jnp.dot(a, b, preferred_element_type=F32)


def build(n_rep, n_z):
    swap = [(0, 1), (1, 0)]

    def per_device(tokens, w_up, d_out, round_k):
        x, w, g = tokens[0], w_up[0], d_out[0]
        toks, rows, ff = x.shape[0], w.shape[0], w.shape[1]
        half = ff // 2
        wide = half // CHUNKS
        z, y = lax.axis_index("z"), lax.axis_index("y")
        mine, other = y * half, (1 - y) * half

        def cols(a, start, width):
            return lax.dynamic_slice(a, (0, start), (a.shape[0], width))

        w_near = lax.ppermute(w, "rep", [(r, r ^ 1) for r in range(n_rep)])
        pieces = []
        for c in range(CHUNKS):
            own = jnp.stack([cols(w, mine + c * wide, wide), cols(w, other + c * wide, wide)])
            near = jnp.stack([cols(w_near, mine + c * wide, wide), cols(w_near, other + c * wide, wide)])
            peer, bit = near, 1
            while 1 << bit < n_rep:
                far = lax.ppermute(own, "rep", [(r, r ^ (1 << bit)) for r in range(n_rep)])
                peer = jnp.where(round_k[0] == bit, far, peer)
                bit += 1
            pieces.append(((own.astype(F32) + peer.astype(F32)) * 0.5).astype(BF16))

        xz = x.reshape(toks, n_z, 2, rows).transpose(1, 0, 2, 3)
        xz = jnp.where(y == 0, xz, xz[:, :, ::-1]).reshape(n_z, toks, 2 * rows)
        xa = lax.all_to_all(xz, "z", 0, 0)
        xb = lax.ppermute(xa, "y", swap)
        xb = jnp.concatenate([xb[..., rows:], xb[..., :rows]], -1)
        xk = jnp.stack([xa, xb], 1).reshape(n_z, 2 * toks, 2 * rows)
        xs = [lax.dynamic_index_in_dim(xk, (z - s) % n_z, 0, keepdims=False) for s in range(n_z)]
        x_all = jnp.concatenate(xs, 0)

        g_other = lax.ppermute(cols(g, other, half), "y", swap)
        g_mine = cols(g, mine, half)

        def right(v, lo, hi):
            return lax.ppermute(v, "z", [(i, i + 1) for i in range(lo, hi)])

        def left(v, lo, hi):
            return lax.ppermute(v, "z", [(n_z - 1 - i, n_z - 2 - i) for i in range(lo, hi)])

        act_out = jnp.zeros((toks, ff), BF16)
        grad_out = jnp.zeros((rows, ff), F32)
        for c in range(CHUNKS):
            avg = pieces[c]
            wc = jnp.concatenate([avg[0], lax.ppermute(avg[1], "y", swap)], 0)
            from_l = from_r = None
            for s in range(1, n_z):
                to_r, to_l = dot(xs[s], wc), dot(xs[n_z - s], wc)
                if s > 1:
                    to_r, to_l = to_r + from_l.astype(F32), to_l + from_r.astype(F32)
                from_l = right(to_r.astype(BF16), 0, s)
                from_r = left(to_l.astype(BF16), 0, s)
            pre = dot(xs[0], wc) + from_l.astype(F32) + from_r.astype(F32)
            act, slope = gelu_parts(pre)
            act = act.astype(BF16)
            gc = jnp.concatenate([g_mine[:, c * wide : (c + 1) * wide], g_other[:, c * wide : (c + 1) * wide]], 0)
            d_pre = (gc.astype(F32) * slope).astype(BF16)
            act_in = lax.ppermute(act[toks:], "y", swap)
            act_out = lax.dynamic_update_slice(act_out, act[:toks], (0, mine + c * wide))
            act_out = lax.dynamic_update_slice(act_out, act_in, (0, other + c * wide))
            got_l, got_r = [d_pre], [d_pre]
            for s in range(1, n_z):
                got_l.append(right(got_l[-1], s - 1, n_z - 1))
                got_r.append(left(got_r[-1], s - 1, n_z - 1))
            ds = [d_pre] + [jnp.where(z >= s, got_l[s], got_r[n_z - s]) for s in range(1, n_z)]
            grad = lax.dot_general(
                x_all, jnp.concatenate(ds, 0), (((0,), (0,)), ((), ())), preferred_element_type=F32
            )
            grad_in = lax.ppermute(grad[rows:].astype(BF16), "y", swap).astype(F32)
            grad_out = lax.dynamic_update_slice(grad_out, grad[:rows], (0, mine + c * wide))
            grad_out = lax.dynamic_update_slice(grad_out, grad_in, (0, other + c * wide))
        return (act_out[None], grad_out[None])

    return per_device


def solution(mesh):
    n_rep, n = mesh.shape["rep"], mesh.shape["fsdp"]
    split = Mesh(mesh.devices.reshape(n_rep, n // 2, 2), ("rep", "z", "y"))
    rows = P("rep", ("z", "y"), None)
    return jax.shard_map(
        build(n_rep, n // 2),
        mesh=split,
        in_specs=(rows, rows, rows, P(("z", "y"))),
        out_specs=(rows, rows),
        check_vma=False,
    )
```
